32 devices in a mesh: rows: 16 (over z, y, x), rep: 2 (over core).
Axes of the slice: x: 2, y: 2, z: 4, core: 2. Of those that a mesh axis runs over, the one named last changes fastest.
Arguments:
- grad_out: bfloat16 [2048, 1024], P('rows'), may hold values from -8 to 8
- w_self: bfloat16 [1024, 1024], replicated, may hold values from -0.1875 to 0.1875
- w_neigh: bfloat16 [1024, 1024], replicated, may hold values from -0.1875 to 0.1875
- adj_tiles: bfloat16 [16, 8, 128, 128], P('rows'), may hold values from -0.3125 to 0.3125
- tile_index: int32 [16, 8], P('rows'), may hold values from 0 to 15, as said below
- tile_count: int32 [16], P('rows'), may hold values from 4 to 8, as said below
- prompt_ids: int32 [2048], P('rows'), may hold values from 0 to 15
Outputs:
- input_grad: bfloat16 [2048, 1024], P('rows')
- prompt_grad: float32 [16, 1024], replicated
The draws below stay inside these ranges and needn't reach their ends.
Inputs may be any that keep to these rules, and one draw needn't show every extreme that they name: `tile_index`: each row holds 8 different tile numbers; only the first tile_count entries of a row are used. `tile_count`: some destination tile uses all 8 slots.
All inputs are finite; a program needn't handle non-finite values.
Results may differ from the reference program's by a relative error of at most 0.0041.
Values may be sent and summed in bfloat16 or wider, within the bound.
A program may use at most 64 MiB of HBM per device.

```python
import math
import jax
import jax.numpy as jnp
from jax import lax

D = 1024
PROMPTS = 16
TILE = 128
NODES = 2048
TILES_ALL = 16
MAXT = 8


def draw_grad_out(key, part):
    base = jax.random.normal(jax.random.fold_in(key, 11), (NODES, D), jnp.float32)
    ramp = jnp.exp(jnp.linspace(math.log(0.5), math.log(1.5), NODES))[:, None]
    values = base * ramp
    return jnp.clip(values, -8.0, 8.0).astype(jnp.bfloat16)


def draw_tile_index(key, part):
    scores = jax.random.randint(jax.random.fold_in(key, 31), (TILES_ALL, TILES_ALL), 0, 2 ** 20)
    scores = scores * TILES_ALL + jnp.arange(TILES_ALL)[None, :]
    ordered = jnp.argsort(scores, axis=1, stable=True)
    return ordered[:, :MAXT].astype(jnp.int32)


def draw_tile_count(key, part):
    drawn = jax.random.randint(jax.random.fold_in(key, 21), (TILES_ALL,), 0, 64)
    counts = 4 + (MAXT - 4) * drawn * drawn // 3969
    chosen = jax.random.randint(jax.random.fold_in(key, 22), (), 0, TILES_ALL)
    counts = jnp.where(jnp.arange(TILES_ALL) == chosen, MAXT, counts)
    return counts.astype(jnp.int32)


def with_ends(result, own_key, low, top_value):
    extent = result.shape
    spot = [jax.random.randint(jax.random.fold_in(own_key, axis), (), 0, extent[axis]) for axis in range(len(extent))]
    result = result.at[tuple(spot)].set(low)
    longest = extent.index(max(extent))
    spot[longest] = (spot[longest] + 1) % extent[longest]
    return result.at[tuple(spot)].set(top_value)


def level_of(key, dims, shards, least, largest):
    def one(dim, parts):
        draws = jax.random.uniform(jax.random.fold_in(jax.random.fold_in(key, 6), dim), (parts,), jnp.float32, least / len(shards), largest / len(shards))
        return jnp.repeat(jnp.exp(draws), dims[dim] // parts).reshape((-1,) + (1,) * (len(dims) - dim - 1))

    factor_of = one(*shards[0])
    for cut in shards[1:]:
        factor_of = factor_of * one(*cut)
    return factor_of


def normal_values(own_key, shape, spread, most, pieces=(), held_as=jnp.bfloat16):
    values = jax.random.normal(own_key, shape, jnp.float32) * spread
    if len(pieces) > 0:
        values = level_of(own_key, shape, pieces, -0.22, 0.18) * values
    return jnp.clip(values, min=-most, max=most).astype(held_as)


def setup_inputs(seed: int = 0) -> dict:
    streams_of = jax.random.split(jax.random.key(seed), 8)
    grad_out = draw_grad_out(jax.random.fold_in(streams_of[7], 71), 0)
    w_self = normal_values(streams_of[1], (D, D), D ** -0.5, 0.1875)
    w_neigh = normal_values(streams_of[2], (D, D), D ** -0.5, 0.1875)
    adj_tiles = normal_values(streams_of[3], (TILES_ALL, MAXT, TILE, TILE), (TILE * MAXT // 3) ** -0.5, 0.3125, ((0, 16),))
    tile_index = draw_tile_index(jax.random.fold_in(streams_of[7], 71), 0)
    tile_count = draw_tile_count(jax.random.fold_in(streams_of[7], 71), 0)
    prompt_ids = with_ends(jax.random.randint(streams_of[6], (NODES,), 0, PROMPTS), jax.random.fold_in(streams_of[6], 1), 0, PROMPTS - 1).astype(jnp.int32)
    return {"grad_out": grad_out, "w_self": w_self, "w_neigh": w_neigh, "adj_tiles": adj_tiles, "tile_index": tile_index, "tile_count": tile_count, "prompt_ids": prompt_ids}


def reference(grad_out, w_self, w_neigh, adj_tiles, tile_index, tile_count, prompt_ids):
    tile_total = adj_tiles.shape[0]
    tile_size = adj_tiles.shape[2]
    width = grad_out.shape[1]
    node_blocks = grad_out.reshape(tile_total, tile_size, width)
    slot_ids = jnp.arange(adj_tiles.shape[1]).astype(jnp.int32)

    def one_tile(inputs):
        tile_set, tile_ids, used_count = inputs
        in_use = (slot_ids < used_count).astype(jnp.float32)
        sources = node_blocks[tile_ids.astype(jnp.int32)].astype(jnp.float32)
        weights_used = tile_set.astype(jnp.float32) * in_use[:, None, None]
        return jnp.einsum("kab,kbf->af", weights_used, sources, precision=lax.Precision.HIGHEST)

    aggregate = lax.map(one_tile, (adj_tiles, tile_index, tile_count))
    aggregate = aggregate.reshape(NODES, width).astype(jnp.bfloat16)
    full_grad = jnp.dot(grad_out, w_self.T, preferred_element_type=jnp.float32)
    full_grad = full_grad + jnp.dot(aggregate, w_neigh.T, preferred_element_type=jnp.float32)
    onehot = (prompt_ids[None, :] == jnp.arange(PROMPTS).astype(jnp.int32)[:, None]).astype(jnp.float32)
    prompt_grad = jnp.dot(onehot, full_grad, precision=lax.Precision.HIGHEST)
    return full_grad.astype(jnp.bfloat16), prompt_grad
```

```python
import functools

import jax
import jax.numpy as jnp
from jax import lax
from jax.experimental import pallas as pl
from jax.experimental.pallas import tpu as pltpu
from jax.sharding import PartitionSpec as P

PROMPTS = 16
LANES = 128
CHUNKS = 2
MESH = pl.DeviceIdType.MESH
NT = (((1,), (1,)), ((), ()))
F32 = jnp.float32
BF16 = jnp.bfloat16


def split_rows(value):
    high = value.astype(BF16)
    low = (value - high.astype(F32)).astype(BF16)
    return jnp.concatenate([high, low], axis=0)


def kernel(
    na, nb, nrep,
    g_ref, ws_hbm, wn_hbm, adj_ref, index_ref, count_ref, ids_ref,
    out_ref, prompt_ref,
    ws, wn, gbuf, asend, arecv, ohsend, ohrecv, psend, precv, pown, agg, acc,
    pv, vsend, vrecv, usend, urecv, fin,
    w_sem, g_send, g_recv, a_send, a_recv, oh_send, oh_recv, p_send, p_recv,
    ag_send, ag_recv, v_send, v_recv, u_send, u_recv, f_send, f_recv,
):
    rows_dev, width = g_ref.shape
    slots = adj_ref.shape[1]
    half = width // nrep
    piece = half // CHUNKS
    group = nb * nrep
    vcols = width // group
    rows = lax.axis_index("rows")
    c = lax.axis_index("rep")
    a, b = rows // nb, rows % nb
    member = b * nrep + c

    load_ws = pltpu.make_async_copy(ws_hbm, ws, w_sem.at[0])
    load_wn = pltpu.make_async_copy(wn_hbm, wn, w_sem.at[1])
    load_ws.start()
    load_wn.start()

    def plane(k):
        return a * nb + (b + k) % nb

    def line(k):
        return (a + k) % na

    barrier = pltpu.get_barrier_semaphore()
    for k in range(1, na):
        pl.semaphore_signal(barrier, inc=1, device_id=(line(k) * nb + b, c), device_id_type=MESH)
    for k in range(1, group):
        other = (member + k) % group
        pl.semaphore_signal(
            barrier, inc=1, device_id=(a * nb + other // nrep, other % nrep), device_id_type=MESH
        )

    base = pl.multiple_of(c * half, half)

    def own_cols(q):
        return pl.ds(pl.multiple_of(base + q * piece, piece), piece)

    for q in range(CHUNKS):
        gbuf[q, pl.ds(pl.multiple_of(a * rows_dev, rows_dev), rows_dev), :] = g_ref[:, own_cols(q)]
    prompt_rows = lax.broadcasted_iota(jnp.int32, (PROMPTS, rows_dev), 0)
    onehot = jnp.where(ids_ref[...] == prompt_rows, 1.0, 0.0).astype(BF16)
    ohsend[...] = onehot
    ohrecv[b] = onehot
    pl.semaphore_wait(barrier, na - 1 + group - 1)

    def g_copy(q, source, step, own):
        place = pl.ds(pl.multiple_of(source * rows_dev, rows_dev), rows_dev)
        return pltpu.make_async_remote_copy(
            src_ref=g_ref.at[:, own_cols(q)] if own else gbuf.at[q, place, :],
            dst_ref=gbuf.at[q, place, :],
            send_sem=g_send.at[q, source, 0 if step > 0 else 1],
            recv_sem=g_recv.at[q, source],
            device_id=((a + step) * nb + b, c),
            device_id_type=MESH,
        )

    up, down = a + 1 < na, a >= 1
    for q in range(CHUNKS):
        @pl.when(up)
        def _():
            g_copy(q, a, 1, True).start()

        @pl.when(down)
        def _():
            g_copy(q, a, -1, True).start()

    def relay(d, q):
        @pl.when(a - d >= 0)
        def _():
            g_copy(q, a - d, 1, False).wait_recv()

            @pl.when(up)
            def _():
                g_copy(q, a - d, 1, False).start()

        @pl.when(a + d < na)
        def _():
            g_copy(q, a + d, -1, False).wait_recv()

            @pl.when(down)
            def _():
                g_copy(q, a + d, -1, False).start()

    def oh_copy(k):
        return pltpu.make_async_remote_copy(
            src_ref=ohsend, dst_ref=ohrecv.at[b], send_sem=oh_send.at[k], recv_sem=oh_recv.at[k],
            device_id=(plane(k), c), device_id_type=MESH,
        )

    def a_copy(k):
        return pltpu.make_async_remote_copy(
            src_ref=asend.at[k], dst_ref=arecv.at[b], send_sem=a_send.at[k], recv_sem=a_recv.at[k],
            device_id=(plane(k), c), device_id_type=MESH,
        )

    used = count_ref[0]

    def block_of(source):
        def look(k, found):
            slot, present = found
            hit = jnp.logical_and(index_ref[0, k] == source, k < used)
            return jnp.where(hit, k, slot), jnp.where(hit, 1.0, present)

        slot, present = lax.fori_loop(
            0, slots, look, (jnp.int32(0), jnp.float32(0.0)), unroll=slots <= 8
        )
        return (adj_ref[0, slot].astype(F32) * present).astype(BF16)

    def spread(ref, place, target):
        def one(j, carry):
            columns = pl.ds(pl.multiple_of(j * rows_dev, rows_dev), rows_dev)
            ref[place, :, columns] = block_of(j * nb + target)
            return carry

        lax.fori_loop(0, na, one, 0)

    for k in range(1, nb):
        oh_copy(k).start()
    for k in range(1, nb):
        spread(asend, k, (b + k) % nb)
        a_copy(k).start()
    spread(arecv, b, b)

    load_ws.wait()
    quarter = width // 4
    for d in range(1, na):
        for q in range(CHUNKS):
            relay(d, q)
        for part in range(4):
            if part * (na - 1) // 4 + 1 == d:
                columns = slice(part * quarter, (part + 1) * quarter)
                acc[:, columns] = lax.dot_general(
                    g_ref[...], ws[columns, :], NT, preferred_element_type=F32
                )

    def p_copy(q, k):
        return pltpu.make_async_remote_copy(
            src_ref=psend.at[q, k], dst_ref=precv.at[q, k],
            send_sem=p_send.at[q, k], recv_sem=p_recv.at[q, k],
            device_id=(plane(k), c), device_id_type=MESH,
        )

    for k in range(1, nb):
        oh_copy(k).wait_recv()
        a_copy(k).wait_recv()
    for q in range(CHUNKS):
        total = jnp.zeros((PROMPTS, piece), F32)
        for k in list(range(1, nb)) + [0]:
            target = (b + k) % nb
            part = jnp.dot(arecv[target], gbuf[q], preferred_element_type=F32)
            high = part.astype(BF16)
            if k:
                psend[q, k] = high
                p_copy(q, k).start()
            else:
                pown[q] = part
            low = (part - high.astype(F32)).astype(BF16)
            hot = ohrecv[target]
            total += jnp.dot(hot, high, preferred_element_type=F32)
            total += jnp.dot(hot, low, preferred_element_type=F32)
        pv[:, q * piece:(q + 1) * piece] = total

    load_wn.wait()
    own_half = pl.ds(base, half)
    own_sum = jnp.dot(ohsend[...], g_ref[:, own_half], preferred_element_type=F32)
    both = lax.dot_general(split_rows(own_sum), ws[:, own_half], NT, preferred_element_type=F32)
    both += lax.dot_general(split_rows(pv[...]), wn[:, own_half], NT, preferred_element_type=F32)
    value = both[:PROMPTS] + both[PROMPTS:]

    def member_id(m):
        return (a * nb + m // nrep, m % nrep)

    for m in range(group):
        vsend[m] = value[:, m * vcols:(m + 1) * vcols]

    def v_copy(k):
        m = (member + k) % group
        return pltpu.make_async_remote_copy(
            src_ref=vsend.at[m], dst_ref=vrecv.at[member], send_sem=v_send.at[k],
            recv_sem=v_recv.at[k], device_id=member_id(m), device_id_type=MESH,
        )

    for k in range(1, group):
        v_copy(k).start()
    vrecv[member] = vsend[member]

    def ag_copy(q, k):
        return pltpu.make_async_remote_copy(
            src_ref=agg.at[c, q], dst_ref=agg.at[c, q], send_sem=ag_send.at[q, k],
            recv_sem=ag_recv.at[q, k], device_id=(rows, (c + k) % nrep), device_id_type=MESH,
        )

    for q in range(CHUNKS):
        total = pown[q]
        for k in range(1, nb):
            p_copy(q, k).wait_recv()
            total += precv[q, k].astype(F32)
        agg[c, q] = total.astype(BF16)
        for k in range(1, nrep):
            ag_copy(q, k).start()

    for k in range(1, group):
        v_copy(k).wait_recv()
    total = vrecv[0]
    for m in range(1, group):
        total += vrecv[m]
    usend[...] = total
    urecv[a] = total

    def u_copy(k):
        return pltpu.make_async_remote_copy(
            src_ref=usend, dst_ref=urecv.at[a], send_sem=u_send.at[k], recv_sem=u_recv.at[k],
            device_id=(line(k) * nb + b, c), device_id_type=MESH,
        )

    for k in range(1, na):
        u_copy(k).start()

    def add_half(r):
        for q in range(CHUNKS):
            columns = pl.ds(pl.multiple_of(r * half + q * piece, piece), piece)
            acc[...] += lax.dot_general(
                agg[r, q], wn[:, columns], NT, preferred_element_type=F32
            )

    add_half(c)
    for k in range(1, nrep):
        for q in range(CHUNKS):
            ag_copy(q, k).wait_recv()
        add_half((c + nrep - k) % nrep)
    out_ref[...] = acc[...].astype(BF16)

    for k in range(1, na):
        u_copy(k).wait_recv()
    total = urecv[0]
    for m in range(1, na):
        total += urecv[m]
    usend2 = fin.at[member]
    fin[member] = total

    def f_copy(k):
        m = (member + k) % group
        return pltpu.make_async_remote_copy(
            src_ref=usend2, dst_ref=fin.at[member], send_sem=f_send.at[k], recv_sem=f_recv.at[k],
            device_id=member_id(m), device_id_type=MESH,
        )

    for k in range(1, group):
        f_copy(k).start()
    for k in range(1, group):
        f_copy(k).wait_recv()
    for m in range(group):
        prompt_ref[:, m * vcols:(m + 1) * vcols] = fin[m]

    for q in range(CHUNKS):
        @pl.when(up)
        def _():
            g_copy(q, a, 1, True).wait_send()

        @pl.when(down)
        def _():
            g_copy(q, a, -1, True).wait_send()

        for d in range(1, na):
            @pl.when(jnp.logical_and(a - d >= 0, up))
            def _():
                g_copy(q, a - d, 1, False).wait_send()

            @pl.when(jnp.logical_and(a + d < na, down))
            def _():
                g_copy(q, a + d, -1, False).wait_send()

        for k in range(1, nb):
            p_copy(q, k).wait_send()
        for k in range(1, nrep):
            ag_copy(q, k).wait_send()
    for k in range(1, nb):
        oh_copy(k).wait_send()
        a_copy(k).wait_send()
    for k in range(1, na):
        u_copy(k).wait_send()
    for k in range(1, group):
        v_copy(k).wait_send()
        f_copy(k).wait_send()


def solution(mesh):
    n, nrep = mesh.shape["rows"], mesh.shape["rep"]

    def shards(grad_out, w_self, w_neigh, adj_tiles, tile_index, tile_count, prompt_ids):
        rows_dev, width = grad_out.shape
        nb = 1
        while n % (2 * nb) == 0 and 4 * nb * nb <= n and width % (2 * nb * nrep * LANES) == 0:
            nb *= 2
        na = n // nb
        half = width // nrep
        piece = half // CHUNKS
        group = nb * nrep
        vcols = width // group
        vmem = pl.BlockSpec(memory_space=pltpu.VMEM)
        smem = pl.BlockSpec(memory_space=pltpu.SMEM)
        hbm = pl.BlockSpec(memory_space=pl.ANY)
        dma = pltpu.SemaphoreType.DMA
        return pl.pallas_call(
            functools.partial(kernel, na, nb, nrep),
            out_shape=(
                jax.ShapeDtypeStruct((rows_dev, width), BF16),
                jax.ShapeDtypeStruct((PROMPTS, width), F32),
            ),
            in_specs=[vmem, hbm, hbm, vmem, smem, smem, vmem],
            out_specs=(vmem, vmem),
            scratch_shapes=[
                pltpu.VMEM((width, width), BF16),
                pltpu.VMEM((width, width), BF16),
                pltpu.VMEM((CHUNKS, na * rows_dev, piece), BF16),
                pltpu.VMEM((nb, rows_dev, na * rows_dev), BF16),
                pltpu.VMEM((nb, rows_dev, na * rows_dev), BF16),
                pltpu.VMEM((PROMPTS, rows_dev), BF16),
                pltpu.VMEM((nb, PROMPTS, rows_dev), BF16),
                pltpu.VMEM((CHUNKS, nb, rows_dev, piece), BF16),
                pltpu.VMEM((CHUNKS, nb, rows_dev, piece), BF16),
                pltpu.VMEM((CHUNKS, rows_dev, piece), F32),
                pltpu.VMEM((nrep, CHUNKS, rows_dev, piece), BF16),
                pltpu.VMEM((rows_dev, width), F32),
                pltpu.VMEM((PROMPTS, half), F32),
                pltpu.VMEM((group, PROMPTS, vcols), F32),
                pltpu.VMEM((group, PROMPTS, vcols), F32),
                pltpu.VMEM((PROMPTS, vcols), F32),
                pltpu.VMEM((na, PROMPTS, vcols), F32),
                pltpu.VMEM((group, PROMPTS, vcols), F32),
                dma((2,)),
                dma((CHUNKS, na, 2)),
                dma((CHUNKS, na)),
                dma((nb,)),
                dma((nb,)),
                dma((nb,)),
                dma((nb,)),
                dma((CHUNKS, nb)),
                dma((CHUNKS, nb)),
                dma((CHUNKS, nrep)),
                dma((CHUNKS, nrep)),
                dma((group,)),
                dma((group,)),
                dma((na,)),
                dma((na,)),
                dma((group,)),
                dma((group,)),
            ],
            compiler_params=pltpu.CompilerParams(
                collective_id=0, has_side_effects=True, vmem_limit_bytes=60 * 2 ** 20
            ),
        )(
            grad_out, w_self, w_neigh, adj_tiles, tile_index, tile_count,
            prompt_ids.reshape(1, rows_dev),
        )

    placed = (
        P("rows", None),
        P(),
        P(),
        P("rows", None, None, None),
        P("rows", None),
        P("rows"),
        P("rows"),
    )
    return jax.shard_map(
        shards, mesh=mesh, in_specs=placed, out_specs=(P("rows", None), P()), check_vma=False
    )
```

```python
import functools

import jax
import jax.numpy as jnp
from jax import lax
from jax.experimental import pallas as pl
from jax.experimental.pallas import tpu as pltpu
from jax.sharding import PartitionSpec as P

PROMPTS = 16
LANES = 128
CHUNKS = 4
MESH = pl.DeviceIdType.MESH
NT = (((1,), (1,)), ((), ()))
F32 = jnp.float32
BF16 = jnp.bfloat16


def split_rows(value):
    high = value.astype(BF16)
    low = (value - high.astype(F32)).astype(BF16)
    return jnp.concatenate([high, low], axis=0)


def kernel(
    na, nb, nrep,
    g_hbm, ws_hbm, wn_hbm, adj_hbm, index_ref, count_ref, ids_ref,
    out_ref, prompt_ref,
    g_ref, adj_ref, ws, wn, gbuf, asend, arecv, ohsend, ohrecv, psend, precv, pown, agg, acc,
    pv, vself, vsend, vrecv, usend, urecv, fin,
    w_sem, g_send, g_recv, a_send, a_recv, fa_send, fa_recv, oh_send, oh_recv, p_send, p_recv,
    ag_send, ag_recv, v_send, v_recv, u_send, u_recv, f_send, f_recv,
):
    rows_dev, width = g_ref.shape
    slots = adj_ref.shape[1]
    share = rows_dev // nrep
    half = width // nrep
    piece = half // CHUNKS
    group = nb * nrep
    vcols = width // group
    rows = lax.axis_index("rows")
    c = lax.axis_index("rep")
    a, b = rows // nb, rows % nb
    member = b * nrep + c

    load_ws = pltpu.make_async_copy(ws_hbm, ws, w_sem.at[0])
    load_wn = pltpu.make_async_copy(wn_hbm, wn, w_sem.at[1])
    load_g = pltpu.make_async_copy(g_hbm, g_ref, w_sem.at[2])
    load_adj = pltpu.make_async_copy(adj_hbm, adj_ref, w_sem.at[3])
    load_g.start()
    load_adj.start()
    load_ws.start()
    load_wn.start()

    def plane(k):
        return a * nb + (b + k) % nb

    def line(k):
        return (a + k) % na

    barrier = pltpu.get_barrier_semaphore()
    for k in range(1, na):
        pl.semaphore_signal(barrier, inc=1, device_id=(line(k) * nb + b, c), device_id_type=MESH)
    for k in range(1, group):
        other = (member + k) % group
        pl.semaphore_signal(
            barrier, inc=1, device_id=(a * nb + other // nrep, other % nrep), device_id_type=MESH
        )

    base = pl.multiple_of(c * half, half)

    def own_cols(q):
        return pl.ds(pl.multiple_of(base + q * piece, piece), piece)

    prompt_rows = lax.broadcasted_iota(jnp.int32, (PROMPTS, rows_dev), 0)
    onehot = jnp.where(ids_ref[...] == prompt_rows, 1.0, 0.0).astype(BF16)
    ohsend[...] = onehot
    ohrecv[b] = onehot
    load_g.wait()
    pl.semaphore_wait(barrier, na - 1 + group - 1)

    def g_copy(q, source, step, own):
        place = pl.ds(pl.multiple_of(source * rows_dev, rows_dev), rows_dev)
        return pltpu.make_async_remote_copy(
            src_ref=g_ref.at[:, own_cols(q)] if own else gbuf.at[q, place, :],
            dst_ref=gbuf.at[q, place, :],
            send_sem=g_send.at[q, source, 0 if step > 0 else 1],
            recv_sem=g_recv.at[q, source],
            device_id=((a + step) * nb + b, c),
            device_id_type=MESH,
        )

    up, down = a + 1 < na, a >= 1

    def send_own(q):
        @pl.when(up)
        def _():
            g_copy(q, a, 1, True).start()

        @pl.when(down)
        def _():
            g_copy(q, a, -1, True).start()

    send_own(0)
    send_own(1)

    def relay(d, q):
        @pl.when(a - d >= 0)
        def _():
            g_copy(q, a - d, 1, False).wait_recv()

            @pl.when(up)
            def _():
                g_copy(q, a - d, 1, False).start()

        @pl.when(a + d < na)
        def _():
            g_copy(q, a + d, -1, False).wait_recv()

            @pl.when(down)
            def _():
                g_copy(q, a + d, -1, False).start()

    def oh_copy(k):
        return pltpu.make_async_remote_copy(
            src_ref=ohsend, dst_ref=ohrecv.at[b], send_sem=oh_send.at[k], recv_sem=oh_recv.at[k],
            device_id=(plane(k), c), device_id_type=MESH,
        )

    my_share = pl.ds(pl.multiple_of(c * share, share), share)

    def a_copy(k):
        return pltpu.make_async_remote_copy(
            src_ref=asend.at[k], dst_ref=arecv.at[b, my_share, :], send_sem=a_send.at[k], recv_sem=a_recv.at[k],
            device_id=(plane(k), c), device_id_type=MESH,
        )

    def fa_copy(k, r):
        source = (b + nb - k) % nb
        return pltpu.make_async_remote_copy(
            src_ref=arecv.at[source, my_share, :], dst_ref=arecv.at[source, my_share, :],
            send_sem=fa_send.at[k, r], recv_sem=fa_recv.at[k, r],
            device_id=(rows, (c + r) % nrep), device_id_type=MESH,
        )

    used = count_ref[0, 0]

    def block_of(source, part):
        def look(k, found):
            slot, present = found
            hit = jnp.logical_and(index_ref[0, k] == source, k < used)
            return jnp.where(hit, k, slot), jnp.where(hit, 1.0, present)

        slot, present = lax.fori_loop(
            0, slots, look, (jnp.int32(0), jnp.float32(0.0)), unroll=slots <= 8
        )
        return (adj_ref[0, slot, part, :].astype(F32) * present).astype(BF16)

    def spread(ref, place, target, part):
        def one(j, carry):
            columns = pl.ds(pl.multiple_of(j * rows_dev, rows_dev), rows_dev)
            ref[place, :, columns] = block_of(j * nb + target, part)
            return carry

        lax.fori_loop(0, na, one, 0)

    for k in range(1, nb):
        oh_copy(k).start()
    load_adj.wait()
    for k in range(1, nb):
        spread(asend, k, (b + k) % nb, my_share)
        a_copy(k).start()
    spread(arecv, b, b, slice(None))
    for q in range(CHUNKS):
        gbuf[q, pl.ds(pl.multiple_of(a * rows_dev, rows_dev), rows_dev), :] = g_ref[:, own_cols(q)]
    load_ws.wait()
    load_wn.wait()
    own_half = pl.ds(base, half)
    quarter = width // 4

    def self_part(part):
        columns = slice(part * quarter, (part + 1) * quarter)
        acc[:, columns] = lax.dot_general(
            g_ref[...], ws[columns, :], NT, preferred_element_type=F32
        )

    def fold(value):
        return value[:PROMPTS] + value[PROMPTS:]

    def self_prompts():
        own_sum = jnp.dot(ohsend[...], g_ref[:, own_half], preferred_element_type=F32)
        vself[...] = fold(lax.dot_general(
            split_rows(own_sum), ws[:, own_half], NT, preferred_element_type=F32
        ))

    def p_copy(q, k):
        return pltpu.make_async_remote_copy(
            src_ref=psend.at[q, k], dst_ref=precv.at[q, k],
            send_sem=p_send.at[q, k], recv_sem=p_recv.at[q, k],
            device_id=(plane(k), c), device_id_type=MESH,
        )

    def partials(q):
        total = jnp.zeros((PROMPTS, piece), F32)
        for k in list(range(1, nb)) + [0]:
            target = (b + k) % nb
            part = jnp.dot(arecv[target], gbuf[q], preferred_element_type=F32)
            high = part.astype(BF16)
            if k:
                psend[q, k] = high
                if q < CHUNKS - 1:
                    p_copy(q, k).start()
            else:
                pown[q] = part
            low = (part - high.astype(F32)).astype(BF16)
            hot = ohrecv[target]
            total += jnp.dot(hot, high, preferred_element_type=F32)
            total += jnp.dot(hot, low, preferred_element_type=F32)
        pv[:, q * piece:(q + 1) * piece] = total

    for t in range(CHUNKS + na - 1):
        if 2 <= t + 1 < CHUNKS:
            send_own(t + 1)
        for d in range(1, na):
            if 0 <= t - d < CHUNKS:
                relay(d, t - d)
        if t == na - 2:
            for k in range(1, nb):
                a_copy(k).wait_recv()
                for r in range(1, nrep):
                    fa_copy(k, r).start()
        for part in range(4):
            if part * (na - 1) // 4 == t:
                self_part(part)
        if t == na - 1:
            self_prompts()
            for k in range(1, nb):
                oh_copy(k).wait_recv()
                for r in range(1, nrep):
                    fa_copy(k, r).wait_recv()
        if t >= na - 1:
            partials(t - na + 1)

    value = vself[...] + fold(lax.dot_general(
        split_rows(pv[...]), wn[:, own_half], NT, preferred_element_type=F32
    ))

    def member_id(m):
        return (a * nb + m // nrep, m % nrep)

    for m in range(group):
        vsend[m] = value[:, m * vcols:(m + 1) * vcols]

    def v_copy(k):
        m = (member + k) % group
        return pltpu.make_async_remote_copy(
            src_ref=vsend.at[m], dst_ref=vrecv.at[member], send_sem=v_send.at[k],
            recv_sem=v_recv.at[k], device_id=member_id(m), device_id_type=MESH,
        )

    for k in range(1, group):
        v_copy(k).start()
    for k in range(1, nb):
        p_copy(CHUNKS - 1, k).start()
    vrecv[member] = vsend[member]

    def ag_copy(q, k):
        return pltpu.make_async_remote_copy(
            src_ref=agg.at[c, q], dst_ref=agg.at[c, q], send_sem=ag_send.at[q, k],
            recv_sem=ag_recv.at[q, k], device_id=(rows, (c + k) % nrep), device_id_type=MESH,
        )

    for q in range(CHUNKS):
        total = pown[q]
        for k in range(1, nb):
            p_copy(q, k).wait_recv()
            total += precv[q, k].astype(F32)
        agg[c, q] = total.astype(BF16)
        for k in range(1, nrep):
            ag_copy(q, k).start()

    for k in range(1, group):
        v_copy(k).wait_recv()
    total = vrecv[0]
    for m in range(1, group):
        total += vrecv[m]
    usend[...] = total
    urecv[a] = total

    def u_copy(k):
        return pltpu.make_async_remote_copy(
            src_ref=usend, dst_ref=urecv.at[a], send_sem=u_send.at[k], recv_sem=u_recv.at[k],
            device_id=(line(k) * nb + b, c), device_id_type=MESH,
        )

    for k in range(1, na):
        u_copy(k).start()

    def add_half(r):
        columns = pl.ds(pl.multiple_of(r * half, half), half)
        joined = jnp.concatenate([agg[r, q] for q in range(CHUNKS)], axis=1)
        acc[...] += lax.dot_general(joined, wn[:, columns], NT, preferred_element_type=F32)

    add_half(c)
    for k in range(1, nrep):
        for q in range(CHUNKS):
            ag_copy(q, k).wait_recv()
        add_half((c + nrep - k) % nrep)
    out_ref[...] = acc[...].astype(BF16)

    for k in range(1, na):
        u_copy(k).wait_recv()
    total = urecv[0]
    for m in range(1, na):
        total += urecv[m]
    usend2 = fin.at[member]
    fin[member] = total

    def f_copy(k):
        m = (member + k) % group
        return pltpu.make_async_remote_copy(
            src_ref=usend2, dst_ref=fin.at[member], send_sem=f_send.at[k], recv_sem=f_recv.at[k],
            device_id=member_id(m), device_id_type=MESH,
        )

    for k in range(1, group):
        f_copy(k).start()
    for k in range(1, group):
        f_copy(k).wait_recv()
    for m in range(group):
        prompt_ref[:, m * vcols:(m + 1) * vcols] = fin[m]

    for q in range(CHUNKS):
        @pl.when(up)
        def _():
            g_copy(q, a, 1, True).wait_send()

        @pl.when(down)
        def _():
            g_copy(q, a, -1, True).wait_send()

        for d in range(1, na):
            @pl.when(jnp.logical_and(a - d >= 0, up))
            def _():
                g_copy(q, a - d, 1, False).wait_send()

            @pl.when(jnp.logical_and(a + d < na, down))
            def _():
                g_copy(q, a + d, -1, False).wait_send()

        for k in range(1, nb):
            p_copy(q, k).wait_send()
        for k in range(1, nrep):
            ag_copy(q, k).wait_send()
    for k in range(1, nb):
        oh_copy(k).wait_send()
        a_copy(k).wait_send()
        for r in range(1, nrep):
            fa_copy(k, r).wait_send()
    for k in range(1, na):
        u_copy(k).wait_send()
    for k in range(1, group):
        v_copy(k).wait_send()
        f_copy(k).wait_send()


def put_out(held_out, held_prompt, out_hbm, prompt_hbm, sem):
    copies = [
        pltpu.make_async_copy(held_out, out_hbm, sem.at[0]),
        pltpu.make_async_copy(held_prompt, prompt_hbm, sem.at[1]),
    ]
    for copy in copies:
        copy.start()
    for copy in copies:
        copy.wait()


def solution(mesh):
    n, nrep = mesh.shape["rows"], mesh.shape["rep"]

    def shards(grad_out, w_self, w_neigh, adj_tiles, tile_index, tile_count, prompt_ids):
        rows_dev, width = grad_out.shape
        nb = 1
        while n % (2 * nb) == 0 and 4 * nb * nb <= n and width % (2 * nb * nrep * LANES) == 0:
            nb *= 2
        na = n // nb
        half = width // nrep
        piece = half // CHUNKS
        group = nb * nrep
        vcols = width // group
        vmem = pl.BlockSpec(memory_space=pltpu.VMEM)
        smem = pl.BlockSpec(memory_space=pltpu.SMEM)
        hbm = pl.BlockSpec(memory_space=pl.ANY)
        dma = pltpu.SemaphoreType.DMA
        held = pl.pallas_call(
            functools.partial(kernel, na, nb, nrep),
            out_shape=(
                pltpu.VMEM((rows_dev, width), BF16),
                pltpu.VMEM((PROMPTS, width), F32),
            ),
            in_specs=[hbm, hbm, hbm, hbm, smem, smem, vmem],
            out_specs=(vmem, vmem),
            scratch_shapes=[
                pltpu.VMEM((rows_dev, width), BF16),
                pltpu.VMEM(adj_tiles.shape, BF16),
                pltpu.VMEM((width, width), BF16),
                pltpu.VMEM((width, width), BF16),
                pltpu.VMEM((CHUNKS, na * rows_dev, piece), BF16),
                pltpu.VMEM((nb, rows_dev // nrep, na * rows_dev), BF16),
                pltpu.VMEM((nb, rows_dev, na * rows_dev), BF16),
                pltpu.VMEM((PROMPTS, rows_dev), BF16),
                pltpu.VMEM((nb, PROMPTS, rows_dev), BF16),
                pltpu.VMEM((CHUNKS, nb, rows_dev, piece), BF16),
                pltpu.VMEM((CHUNKS, nb, rows_dev, piece), BF16),
                pltpu.VMEM((CHUNKS, rows_dev, piece), F32),
                pltpu.VMEM((nrep, CHUNKS, rows_dev, piece), BF16),
                pltpu.VMEM((rows_dev, width), F32),
                pltpu.VMEM((PROMPTS, half), F32),
                pltpu.VMEM((PROMPTS, width), F32),
                pltpu.VMEM((group, PROMPTS, vcols), F32),
                pltpu.VMEM((group, PROMPTS, vcols), F32),
                pltpu.VMEM((PROMPTS, vcols), F32),
                pltpu.VMEM((na, PROMPTS, vcols), F32),
                pltpu.VMEM((group, PROMPTS, vcols), F32),
                dma((4,)),
                dma((CHUNKS, na, 2)),
                dma((CHUNKS, na)),
                dma((nb,)),
                dma((nb,)),
                dma((nb, nrep)),
                dma((nb, nrep)),
                dma((nb,)),
                dma((nb,)),
                dma((CHUNKS, nb)),
                dma((CHUNKS, nb)),
                dma((CHUNKS, nrep)),
                dma((CHUNKS, nrep)),
                dma((group,)),
                dma((group,)),
                dma((na,)),
                dma((na,)),
                dma((group,)),
                dma((group,)),
            ],
            compiler_params=pltpu.CompilerParams(
                collective_id=0, has_side_effects=True, vmem_limit_bytes=56 * 2 ** 20
            ),
        )(
            grad_out, w_self, w_neigh, adj_tiles, tile_index, tile_count.reshape(1, 1),
            prompt_ids.reshape(1, rows_dev),
        )
        return pl.pallas_call(
            put_out,
            out_shape=(
                jax.ShapeDtypeStruct((rows_dev, width), BF16),
                jax.ShapeDtypeStruct((PROMPTS, width), F32),
            ),
            in_specs=[vmem, vmem],
            out_specs=(hbm, hbm),
            scratch_shapes=[dma((2,))],
            compiler_params=pltpu.CompilerParams(vmem_limit_bytes=2 ** 20),
        )(*held)

    placed = (
        P("rows", None),
        P(),
        P(),
        P("rows", None, None, None),
        P("rows", None),
        P("rows"),
        P("rows"),
    )
    return jax.shard_map(
        shards, mesh=mesh, in_specs=placed, out_specs=(P("rows", None), P()), check_vma=False
    )
```

```python
import functools

import jax
import jax.numpy as jnp
from jax import lax
from jax.experimental import pallas as pl
from jax.experimental.pallas import tpu as pltpu
from jax.sharding import PartitionSpec as P

PROMPTS = 16
LANES = 128
CHUNKS = 4
MESH = pl.DeviceIdType.MESH
NT = (((1,), (1,)), ((), ()))
F32 = jnp.float32
BF16 = jnp.bfloat16


def split_rows(value):
    high = value.astype(BF16)
    low = (value - high.astype(F32)).astype(BF16)
    return jnp.concatenate([high, low], axis=0)


def kernel(
    na, nb, nrep,
    g_hbm, ws_hbm, wn_hbm, adj_hbm, index_ref, count_ref, ids_ref,
    out_ref, prompt_ref,
    g_ref, adj_ref, ws, wn, gbuf, asend, arecv, ohsend, ohrecv, psend, precv, pown, agg, acc,
    csend, crecv, vself, vsend, vrecv, usend, urecv, fin,
    w_sem, g_send, g_recv, a_send, a_recv, fa_send, fa_recv, oh_send, oh_recv, p_send, p_recv,
    ag_send, ag_recv, c_send, c_recv, v_send, v_recv, u_send, u_recv, f_send, f_recv,
):
    rows_dev, width = g_ref.shape
    slots = adj_ref.shape[1]
    share = rows_dev // nrep
    half = width // nrep
    piece = half // CHUNKS
    group = nb * nrep
    vcols = width // group
    rows = lax.axis_index("rows")
    c = lax.axis_index("rep")
    a, b = rows // nb, rows % nb
    member = b * nrep + c

    load_ws = pltpu.make_async_copy(ws_hbm, ws, w_sem.at[0])
    load_wn = pltpu.make_async_copy(wn_hbm, wn, w_sem.at[1])
    load_g = pltpu.make_async_copy(g_hbm, g_ref, w_sem.at[2])
    load_adj = pltpu.make_async_copy(adj_hbm, adj_ref, w_sem.at[3])
    load_g.start()
    load_adj.start()
    load_ws.start()
    load_wn.start()

    def plane(k):
        return a * nb + (b + k) % nb

    def line(k):
        return (a + k) % na

    barrier = pltpu.get_barrier_semaphore()
    for k in range(1, na):
        pl.semaphore_signal(barrier, inc=1, device_id=(line(k) * nb + b, c), device_id_type=MESH)
    for k in range(1, group):
        other = (member + k) % group
        pl.semaphore_signal(
            barrier, inc=1, device_id=(a * nb + other // nrep, other % nrep), device_id_type=MESH
        )

    base = pl.multiple_of(c * half, half)

    def own_cols(q):
        return pl.ds(pl.multiple_of(base + q * piece, piece), piece)

    prompt_rows = lax.broadcasted_iota(jnp.int32, (PROMPTS, rows_dev), 0)
    onehot = jnp.where(ids_ref[...] == prompt_rows, 1.0, 0.0).astype(BF16)
    ohsend[...] = onehot
    ohrecv[b] = onehot
    load_g.wait()
    pl.semaphore_wait(barrier, na - 1 + group - 1)

    def g_copy(q, source, step, own):
        place = pl.ds(pl.multiple_of(source * rows_dev, rows_dev), rows_dev)
        return pltpu.make_async_remote_copy(
            src_ref=g_ref.at[:, own_cols(q)] if own else gbuf.at[q, place, :],
            dst_ref=gbuf.at[q, place, :],
            send_sem=g_send.at[q, source, 0 if step > 0 else 1],
            recv_sem=g_recv.at[q, source],
            device_id=((a + step) * nb + b, c),
            device_id_type=MESH,
        )

    up, down = a + 1 < na, a >= 1

    def send_own(q):
        @pl.when(up)
        def _():
            g_copy(q, a, 1, True).start()

        @pl.when(down)
        def _():
            g_copy(q, a, -1, True).start()

    for q in range(CHUNKS):
        send_own(q)

    def relay(d, q):
        @pl.when(a - d >= 0)
        def _():
            g_copy(q, a - d, 1, False).wait_recv()

            @pl.when(up)
            def _():
                g_copy(q, a - d, 1, False).start()

        @pl.when(a + d < na)
        def _():
            g_copy(q, a + d, -1, False).wait_recv()

            @pl.when(down)
            def _():
                g_copy(q, a + d, -1, False).start()

    def oh_copy(k):
        return pltpu.make_async_remote_copy(
            src_ref=ohsend, dst_ref=ohrecv.at[b], send_sem=oh_send.at[k], recv_sem=oh_recv.at[k],
            device_id=(plane(k), c), device_id_type=MESH,
        )

    my_share = pl.ds(pl.multiple_of(c * share, share), share)

    def a_copy(k):
        return pltpu.make_async_remote_copy(
            src_ref=asend.at[k], dst_ref=arecv.at[b, my_share, :], send_sem=a_send.at[k], recv_sem=a_recv.at[k],
            device_id=(plane(k), c), device_id_type=MESH,
        )

    def fa_copy(k, r):
        source = (b + nb - k) % nb
        return pltpu.make_async_remote_copy(
            src_ref=arecv.at[source, my_share, :], dst_ref=arecv.at[source, my_share, :],
            send_sem=fa_send.at[k, r], recv_sem=fa_recv.at[k, r],
            device_id=(rows, (c + r) % nrep), device_id_type=MESH,
        )

    used = count_ref[0, 0]

    def block_of(source, part):
        def look(k, found):
            slot, present = found
            hit = jnp.logical_and(index_ref[0, k] == source, k < used)
            return jnp.where(hit, k, slot), jnp.where(hit, 1.0, present)

        slot, present = lax.fori_loop(
            0, slots, look, (jnp.int32(0), jnp.float32(0.0)), unroll=slots <= 8
        )
        return (adj_ref[0, slot, part, :].astype(F32) * present).astype(BF16)

    def spread(ref, place, target, part):
        def one(j, carry):
            columns = pl.ds(pl.multiple_of(j * rows_dev, rows_dev), rows_dev)
            ref[place, :, columns] = block_of(j * nb + target, part)
            return carry

        lax.fori_loop(0, na, one, 0)

    for k in range(1, nb):
        oh_copy(k).start()
    load_adj.wait()
    for k in range(1, nb):
        spread(asend, k, (b + k) % nb, my_share)
        a_copy(k).start()
    spread(arecv, b, b, slice(None))
    for q in range(CHUNKS):
        gbuf[q, pl.ds(pl.multiple_of(a * rows_dev, rows_dev), rows_dev), :] = g_ref[:, own_cols(q)]
    load_ws.wait()
    load_wn.wait()
    own_half = pl.ds(base, half)
    quarter = width // 4

    def self_part(part):
        columns = slice(part * quarter, (part + 1) * quarter)
        acc[:, columns] = lax.dot_general(
            g_ref[...], ws[columns, :], NT, preferred_element_type=F32
        )

    def fold(value):
        return value[:PROMPTS] + value[PROMPTS:]

    def self_prompts():
        own_sum = jnp.dot(ohsend[...], g_ref[:, own_half], preferred_element_type=F32)
        vself[...] = fold(lax.dot_general(
            split_rows(own_sum), ws[:, own_half], NT, preferred_element_type=F32
        ))

    def p_copy(q, k):
        return pltpu.make_async_remote_copy(
            src_ref=psend.at[q, k], dst_ref=precv.at[q, k],
            send_sem=p_send.at[q, k], recv_sem=p_recv.at[q, k],
            device_id=(plane(k), c), device_id_type=MESH,
        )

    def partials(q):
        for k in list(range(1, nb)) + [0]:
            part = jnp.dot(arecv[(b + k) % nb], gbuf[q], preferred_element_type=F32)
            if k:
                psend[q, k] = part.astype(BF16)
                p_copy(q, k).start()
            else:
                pown[q] = part

    def c_copy(k):
        return pltpu.make_async_remote_copy(
            src_ref=csend.at[line(k)], dst_ref=crecv.at[a], send_sem=c_send.at[k],
            recv_sem=c_recv.at[k], device_id=(line(k) * nb + b, c), device_id_type=MESH,
        )

    def send_coefficients():
        total = jnp.zeros((PROMPTS, na * rows_dev), F32)
        for k in range(nb):
            total += jnp.dot(ohrecv[k], arecv[k], preferred_element_type=F32)
        for m in range(na):
            csend[m] = total[:, m * rows_dev:(m + 1) * rows_dev]
        for k in range(1, na):
            c_copy(k).start()
        crecv[a] = csend[a]

    def member_id(m):
        return (a * nb + m // nrep, m % nrep)

    def v_copy(k):
        m = (member + k) % group
        return pltpu.make_async_remote_copy(
            src_ref=vsend.at[m], dst_ref=vrecv.at[member], send_sem=v_send.at[k],
            recv_sem=v_recv.at[k], device_id=member_id(m), device_id_type=MESH,
        )

    def send_prompts():
        for k in range(1, na):
            c_copy(k).wait_recv()
        total = crecv[0]
        for m in range(1, na):
            total += crecv[m]
        through = fold(jnp.dot(split_rows(total), g_ref[:, own_half], preferred_element_type=F32))
        value = vself[...] + fold(lax.dot_general(
            split_rows(through), wn[:, own_half], NT, preferred_element_type=F32
        ))
        for m in range(group):
            vsend[m] = value[:, m * vcols:(m + 1) * vcols]
        for k in range(1, group):
            v_copy(k).start()
        vrecv[member] = vsend[member]

    for t in range(CHUNKS + na - 1):
        for d in range(1, na):
            if 0 <= t - d < CHUNKS:
                relay(d, t - d)
        if t == na - 2:
            for k in range(1, nb):
                a_copy(k).wait_recv()
                for r in range(1, nrep):
                    fa_copy(k, r).start()
        for part in range(4):
            if part * (na - 1) // 4 == t:
                self_part(part)
        if t == na - 1:
            self_prompts()
            for k in range(1, nb):
                oh_copy(k).wait_recv()
                for r in range(1, nrep):
                    fa_copy(k, r).wait_recv()
            send_coefficients()
        if t >= na - 1:
            partials(t - na + 1)
        if t == CHUNKS + na - 3:
            send_prompts()

    def ag_copy(q, k):
        return pltpu.make_async_remote_copy(
            src_ref=agg.at[c, q], dst_ref=agg.at[c, q], send_sem=ag_send.at[q, k],
            recv_sem=ag_recv.at[q, k], device_id=(rows, (c + k) % nrep), device_id_type=MESH,
        )

    for k in range(1, group):
        v_copy(k).wait_recv()
    total = vrecv[0]
    for m in range(1, group):
        total += vrecv[m]
    usend[...] = total
    urecv[a] = total

    def u_copy(k):
        return pltpu.make_async_remote_copy(
            src_ref=usend, dst_ref=urecv.at[a], send_sem=u_send.at[k], recv_sem=u_recv.at[k],
            device_id=(line(k) * nb + b, c), device_id_type=MESH,
        )

    for k in range(1, na):
        u_copy(k).start()

    for q in range(CHUNKS):
        total = pown[q]
        for k in range(1, nb):
            p_copy(q, k).wait_recv()
            total += precv[q, k].astype(F32)
        agg[c, q] = total.astype(BF16)
        for k in range(1, nrep):
            ag_copy(q, k).start()

    def add_half(r):
        columns = pl.ds(pl.multiple_of(r * half, half), half)
        joined = jnp.concatenate([agg[r, q] for q in range(CHUNKS)], axis=1)
        acc[...] += lax.dot_general(joined, wn[:, columns], NT, preferred_element_type=F32)

    add_half(c)
    for k in range(1, na):
        u_copy(k).wait_recv()
    total = urecv[0]
    for m in range(1, na):
        total += urecv[m]
    usend2 = fin.at[member]
    fin[member] = total

    def f_copy(k):
        m = (member + k) % group
        return pltpu.make_async_remote_copy(
            src_ref=usend2, dst_ref=fin.at[member], send_sem=f_send.at[k], recv_sem=f_recv.at[k],
            device_id=member_id(m), device_id_type=MESH,
        )

    for k in range(1, group):
        f_copy(k).start()
    for k in range(1, nrep):
        for q in range(CHUNKS):
            ag_copy(q, k).wait_recv()
        add_half((c + nrep - k) % nrep)
    out_ref[...] = acc[...].astype(BF16)

    for k in range(1, group):
        f_copy(k).wait_recv()
    for m in range(group):
        prompt_ref[:, m * vcols:(m + 1) * vcols] = fin[m]

    for q in range(CHUNKS):
        @pl.when(up)
        def _():
            g_copy(q, a, 1, True).wait_send()

        @pl.when(down)
        def _():
            g_copy(q, a, -1, True).wait_send()

        for d in range(1, na):
            @pl.when(jnp.logical_and(a - d >= 0, up))
            def _():
                g_copy(q, a - d, 1, False).wait_send()

            @pl.when(jnp.logical_and(a + d < na, down))
            def _():
                g_copy(q, a + d, -1, False).wait_send()

        for k in range(1, nb):
            p_copy(q, k).wait_send()
        for k in range(1, nrep):
            ag_copy(q, k).wait_send()
    for k in range(1, nb):
        oh_copy(k).wait_send()
        a_copy(k).wait_send()
        for r in range(1, nrep):
            fa_copy(k, r).wait_send()
    for k in range(1, na):
        c_copy(k).wait_send()
        u_copy(k).wait_send()
    for k in range(1, group):
        v_copy(k).wait_send()
        f_copy(k).wait_send()


def put_out(held_out, held_prompt, out_hbm, prompt_hbm, sem):
    copies = [
        pltpu.make_async_copy(held_out, out_hbm, sem.at[0]),
        pltpu.make_async_copy(held_prompt, prompt_hbm, sem.at[1]),
    ]
    for copy in copies:
        copy.start()
    for copy in copies:
        copy.wait()


def solution(mesh):
    n, nrep = mesh.shape["rows"], mesh.shape["rep"]

    def shards(grad_out, w_self, w_neigh, adj_tiles, tile_index, tile_count, prompt_ids):
        rows_dev, width = grad_out.shape
        nb = 1
        while n % (2 * nb) == 0 and 4 * nb * nb <= n and width % (2 * nb * nrep * LANES) == 0:
            nb *= 2
        na = n // nb
        half = width // nrep
        piece = half // CHUNKS
        group = nb * nrep
        vcols = width // group
        vmem = pl.BlockSpec(memory_space=pltpu.VMEM)
        smem = pl.BlockSpec(memory_space=pltpu.SMEM)
        hbm = pl.BlockSpec(memory_space=pl.ANY)
        dma = pltpu.SemaphoreType.DMA
        held = pl.pallas_call(
            functools.partial(kernel, na, nb, nrep),
            out_shape=(
                pltpu.VMEM((rows_dev, width), BF16),
                pltpu.VMEM((PROMPTS, width), F32),
            ),
            in_specs=[hbm, hbm, hbm, hbm, smem, smem, vmem],
            out_specs=(vmem, vmem),
            scratch_shapes=[
                pltpu.VMEM((rows_dev, width), BF16),
                pltpu.VMEM(adj_tiles.shape, BF16),
                pltpu.VMEM((width, width), BF16),
                pltpu.VMEM((width, width), BF16),
                pltpu.VMEM((CHUNKS, na * rows_dev, piece), BF16),
                pltpu.VMEM((nb, rows_dev // nrep, na * rows_dev), BF16),
                pltpu.VMEM((nb, rows_dev, na * rows_dev), BF16),
                pltpu.VMEM((PROMPTS, rows_dev), BF16),
                pltpu.VMEM((nb, PROMPTS, rows_dev), BF16),
                pltpu.VMEM((CHUNKS, nb, rows_dev, piece), BF16),
                pltpu.VMEM((CHUNKS, nb, rows_dev, piece), BF16),
                pltpu.VMEM((CHUNKS, rows_dev, piece), F32),
                pltpu.VMEM((nrep, CHUNKS, rows_dev, piece), BF16),
                pltpu.VMEM((rows_dev, width), F32),
                pltpu.VMEM((na, PROMPTS, rows_dev), F32),
                pltpu.VMEM((na, PROMPTS, rows_dev), F32),
                pltpu.VMEM((PROMPTS, width), F32),
                pltpu.VMEM((group, PROMPTS, vcols), F32),
                pltpu.VMEM((group, PROMPTS, vcols), F32),
                pltpu.VMEM((PROMPTS, vcols), F32),
                pltpu.VMEM((na, PROMPTS, vcols), F32),
                pltpu.VMEM((group, PROMPTS, vcols), F32),
                dma((4,)),
                dma((CHUNKS, na, 2)),
                dma((CHUNKS, na)),
                dma((nb,)),
                dma((nb,)),
                dma((nb, nrep)),
                dma((nb, nrep)),
                dma((nb,)),
                dma((nb,)),
                dma((CHUNKS, nb)),
                dma((CHUNKS, nb)),
                dma((CHUNKS, nrep)),
                dma((CHUNKS, nrep)),
                dma((na,)),
                dma((na,)),
                dma((group,)),
                dma((group,)),
                dma((na,)),
                dma((na,)),
                dma((group,)),
                dma((group,)),
            ],
            compiler_params=pltpu.CompilerParams(
                collective_id=0, has_side_effects=True, vmem_limit_bytes=56 * 2 ** 20
            ),
        )(
            grad_out, w_self, w_neigh, adj_tiles, tile_index, tile_count.reshape(1, 1),
            prompt_ids.reshape(1, rows_dev),
        )
        return pl.pallas_call(
            put_out,
            out_shape=(
                jax.ShapeDtypeStruct((rows_dev, width), BF16),
                jax.ShapeDtypeStruct((PROMPTS, width), F32),
            ),
            in_specs=[vmem, vmem],
            out_specs=(hbm, hbm),
            scratch_shapes=[dma((2,))],
            compiler_params=pltpu.CompilerParams(vmem_limit_bytes=2 ** 20),
        )(*held)

    placed = (
        P("rows", None),
        P(),
        P(),
        P("rows", None, None, None),
        P("rows", None),
        P("rows"),
        P("rows"),
    )
    return jax.shard_map(
        shards, mesh=mesh, in_specs=placed, out_specs=(P("rows", None), P()), check_vma=False
    )
```
